32 devices in a mesh: chan: 8 (over z, core), rad: 4 (over y, x).
Axes of the slice: x: 2, y: 2, z: 4, core: 2. Of those that a mesh axis runs over, the one named last changes fastest.
Arguments:
- wave_field: float32 [2, 128, 32, 1024], P(None, 'chan', 'rad'), may hold values from -6 to 6
- partner: int32 [128, 8], replicated, may hold values from 0 to 127, as said below
- coupling_kind: int32 [128, 8], replicated, may hold values from 0 to 3
- coupling: float32 [128, 8], replicated, may hold values from -1 to 1
- angular: int32 [128, 2], replicated, may hold values from 0 to 11
Outputs:
- advanced: float32 [2, 128, 32, 1024], P(None, 'chan', 'rad')
The draws below stay inside these ranges and needn't reach their ends.
Inputs may be any that keep to these rules, and one draw needn't show every extreme that they name: partner[c, s] differs from c by at most 8; entry 0 of every channel lies exactly 8 away and entry 1 is the channel itself.
All inputs are finite; a program needn't handle non-finite values.
Results may differ from the reference program's by a relative error of at most 0.0003.
Values sent between devices are 32-bit elements; how exact they have to be, the bound alone decides.
A program may use at most 64 MiB of HBM per device.

```python
import jax
import jax.numpy as jnp
from jax import lax

CH_DEV = 16
NB = 8
KINDS = 4
NR2 = 1024
REACH = 8
CHANNELS = 128
NR1 = 32


def draw_partner(key, part):
    channel = jnp.arange(CHANNELS).astype(jnp.int32)[:, None]
    offsets = jax.random.randint(key, (CHANNELS, NB - 2), -REACH, REACH + 1).astype(jnp.int32)
    first_entry = jnp.where(channel + REACH < CHANNELS, REACH, -REACH).astype(jnp.int32)
    self_entry = jnp.zeros((CHANNELS, 1), jnp.int32)
    offsets = jnp.concatenate([first_entry, self_entry, offsets], axis=1)
    return jnp.clip(channel + offsets, 0, CHANNELS - 1).astype(jnp.int32)


def touch_ends(values, stream_key, low, top_value):
    spot = [jax.random.randint(jax.random.fold_in(stream_key, axis), (), 0, length) for axis, length in enumerate(values.shape)]
    main_axis = values.shape.index(max(values.shape))
    next_to = spot[:main_axis] + [(spot[main_axis] + 1) % values.shape[main_axis]] + spot[main_axis + 1:]
    return values.at[tuple(spot)].set(low).at[tuple(next_to)].set(top_value)


def block_levels(own_key, extent, split, low, top_value):
    gain = 1.0
    for dim, blocks in split:
        heights = jax.random.uniform(jax.random.fold_in(jax.random.fold_in(own_key, 6), dim), (blocks,), jnp.float32, low / len(split), top_value / len(split))
        gain = gain * jnp.repeat(jnp.exp(heights), extent[dim] // blocks).reshape((-1,) + (1,) * (len(extent) - 1 - dim))
    return gain


def bell_draw(stream_key, dims, width, reach, cuts=(), dtype=jnp.bfloat16):
    array = width * jax.random.normal(stream_key, dims, jnp.float32)
    if cuts:
        array = array * block_levels(stream_key, dims, cuts, -0.22, 0.18)
    return jnp.clip(array, -reach, reach).astype(dtype)


def setup_inputs(seed: int = 0) -> dict:
    splits = jax.random.split(jax.random.key(seed), 6)
    return {
        "wave_field": bell_draw(splits[0], (2, CHANNELS, NR1, NR2), 1.0, 6.0, ((1, 8), (2, 4)), jnp.float32),
        "partner": draw_partner(jax.random.fold_in(splits[5], 71), 0),
        "coupling_kind": touch_ends(jax.random.randint(splits[2], (CHANNELS, NB), 0, KINDS), jax.random.fold_in(splits[2], 1), 0, KINDS - 1).astype(jnp.int32),
        "coupling": bell_draw(splits[3], (CHANNELS, NB), 0.25, 1.0, (), jnp.float32),
        "angular": touch_ends(jax.random.randint(splits[4], (CHANNELS, 2), 0, 12), jax.random.fold_in(splits[4], 1), 0, 11).astype(jnp.int32),
    }


time_step = 0.004
grid_step = 0.2
radius_start = 1.0


def radial_forms(radius_one, radius_two):
    greater = jnp.maximum(radius_one, radius_two)
    lesser = jnp.minimum(radius_one, radius_two)
    shape = greater.shape
    return [jnp.broadcast_to(radius_one, shape), jnp.broadcast_to(radius_two, shape), 1.0 / greater, lesser / (greater * greater)]


def hamiltonian(field, partner, coupling_kind, coupling, angular):
    nrows = field.shape[2]
    ncols = field.shape[3]
    radius_one = radius_start + grid_step * jnp.arange(nrows).astype(jnp.float32)
    radius_two = radius_start + grid_step * jnp.arange(ncols).astype(jnp.float32)
    factors = jnp.stack(radial_forms(radius_one[:, None], radius_two[None, :]))

    def block(index):
        start = (index * CH_DEV).astype(jnp.int32)
        own = lax.dynamic_slice_in_dim(field, start, CH_DEV, 1)
        links = lax.dynamic_slice_in_dim(partner, start, CH_DEV, 0)
        kinds = lax.dynamic_slice_in_dim(coupling_kind, start, CH_DEV, 0)
        coeffs = lax.dynamic_slice_in_dim(coupling, start, CH_DEV, 0)
        ells = lax.dynamic_slice_in_dim(angular, start, CH_DEV, 0).astype(jnp.float32)
        padded = jnp.pad(own, ((0, 0), (0, 0), (2, 2), (2, 2)))
        mid = padded[:, :, :, 2:-2]
        d_rows = -mid[:, :, 0:nrows] + 16.0 * mid[:, :, 1:nrows + 1] - 30.0 * own + 16.0 * mid[:, :, 3:nrows + 3] - mid[:, :, 4:nrows + 4]
        side = padded[:, :, 2:-2, :]
        d_cols = -side[..., 0:ncols] + 16.0 * side[..., 1:ncols + 1] - 30.0 * own + 16.0 * side[..., 3:ncols + 3] - side[..., 4:ncols + 4]
        kinetic = -(d_rows + d_cols) / (24.0 * grid_step * grid_step)
        spin = ells * (ells + 1.0)
        barrier = spin[:, 0][:, None, None] * (0.5 / (radius_one * radius_one))[None, :, None] + spin[:, 1][:, None, None] * (0.5 / (radius_two * radius_two))[None, None, :]
        result = kinetic + barrier[None] * own
        for entry in range(NB):
            picked = jnp.take(field, links[:, entry], axis=1)
            weights = coeffs[:, entry][:, None] * (kinds[:, entry][:, None] == jnp.arange(KINDS)[None, :]).astype(jnp.float32)
            scale = jnp.einsum('ck,kxy->cxy', weights, factors, precision=lax.Precision.HIGHEST)
            result = result + scale[None] * picked
        return result

    count = field.shape[1] // CH_DEV
    blocks = lax.map(block, jnp.arange(count).astype(jnp.int32))
    return jnp.moveaxis(blocks, 0, 1).reshape(field.shape)


def rotate(applied):
    return time_step * jnp.stack([applied[1], -applied[0]])


def reference(wave_field, partner, coupling_kind, coupling, angular):
    first = rotate(hamiltonian(wave_field, partner, coupling_kind, coupling, angular))
    second = rotate(hamiltonian(first, partner, coupling_kind, coupling, angular))
    return wave_field + first + 0.5 * second
```

```python
import functools

import jax
import jax.numpy as jnp
from jax import lax
from jax.experimental import pallas as pl
from jax.experimental.pallas import tpu as pltpu
from jax.sharding import PartitionSpec as P

KINDS = 4

time_step = 0.004
grid_step = 0.2
radius_start = 1.0
kinetic_scale = -1.0 / (24.0 * grid_step * grid_step)

RIGHT, LEFT, DOWN, UP, DOWN_HI, UP_HI, RELAY, FORWARD = range(8)


def kernel(
    partner_ref, kind_ref, coef_ref, angular_ref, wave_ref, out_ref,
    links, kinds, coefs, angulars, forms,
    ext_w0, ext_w1, ext_f1, ext_f0, base_a, base_b, pack, above, below, relay,
    table_sem, local_sem, send_sem, recv_sem,
):
    nchan, nrows, ncols = wave_ref.shape[1:]
    nentries = coef_ref.shape[0]
    reach = nchan // 2
    group = nrows // 2
    chan, rad = lax.axis_index("chan"), lax.axis_index("rad")
    chans, rads = lax.axis_size("chan"), lax.axis_size("rad")
    chan_start = chan * nchan
    has = {RIGHT: chan < chans - 1, LEFT: chan > 0, DOWN: rad < rads - 1, UP: rad > 0}
    target = {
        RIGHT: {"chan": chan + 1}, LEFT: {"chan": chan - 1},
        DOWN: {"rad": rad + 1}, UP: {"rad": rad - 1},
    }
    opposite = {RIGHT: LEFT, LEFT: RIGHT, DOWN: UP, UP: DOWN}
    own = pl.ds(reach, nchan)
    exts = (ext_w0, ext_w1, ext_f1, ext_f0)

    barrier = pltpu.get_barrier_semaphore()
    for way in range(4):
        @pl.when(has[way])
        def _():
            pl.semaphore_signal(
                barrier, inc=1, device_id=target[way], device_id_type=pl.DeviceIdType.MESH
            )
    relayed = rads == 4
    across = {"rad": lax.rem(rad + 2, rads)}
    if relayed:
        pl.semaphore_signal(barrier, inc=1, device_id=across, device_id_type=pl.DeviceIdType.MESH)

    fills = [
        pltpu.make_async_copy(wave_ref.at[p], exts[p].at[own], local_sem.at[p]) for p in range(2)
    ]
    tables = [
        pltpu.make_async_copy(src, dst, table_sem.at[i])
        for i, (src, dst) in enumerate(
            ((partner_ref, links), (kind_ref, kinds), (coef_ref, coefs), (angular_ref, angulars))
        )
    ]
    for copy in fills + tables:
        copy.start()

    def remote(source, dest, phase, sent, received, device):
        return pltpu.make_async_remote_copy(
            src_ref=source, dst_ref=dest,
            send_sem=send_sem.at[phase, sent], recv_sem=recv_sem.at[phase, received],
            device_id=device, device_id_type=pl.DeviceIdType.MESH,
        )

    half = nchan // group // 2
    low, high = pl.ds(0, half), pl.ds(half, half)

    def copy_of(phase, way):
        ext = exts[phase]
        if way == RIGHT:
            source = wave_ref.at[phase, pl.ds(reach, reach)] if phase < 2 else ext.at[pl.ds(nchan, reach)]
            dest = ext.at[pl.ds(0, reach)]
        elif way == LEFT:
            source = wave_ref.at[phase, pl.ds(0, reach)] if phase < 2 else ext.at[pl.ds(reach, reach)]
            dest = ext.at[pl.ds(reach + nchan, reach)]
        elif way == DOWN:
            source, dest = pack.at[phase, 0, low], above.at[phase, low]
        elif way == UP:
            source, dest = pack.at[phase, 1, low], below.at[phase, low]
        elif way == DOWN_HI:
            source, dest = pack.at[phase, 0, high], above.at[phase, high]
        else:
            source, dest = pack.at[phase, 1, high], below.at[phase, high]
        toward = {DOWN_HI: DOWN, UP_HI: UP}.get(way, way)
        return remote(source, dest, phase, way, way, target[toward])

    def to_relay(phase, way):
        side = 0 if way == DOWN_HI else 1
        return remote(pack.at[phase, side, high], relay.at[phase], phase, way, RELAY, across)

    middle = {DOWN_HI: rad == 1, UP_HI: rad == 2}

    def send_one(phase, way):
        if way in middle:
            direct = has[DOWN if way == DOWN_HI else UP]
            if relayed:
                direct = jnp.logical_and(direct, jnp.logical_not(middle[way]))

                @pl.when(middle[way])
                def _():
                    to_relay(phase, way).start()
        else:
            direct = has[way]

        @pl.when(direct)
        def _():
            copy_of(phase, way).start()

    def send_rows(phase):
        for way in (DOWN, UP, DOWN_HI, UP_HI):
            send_one(phase, way)

    def send_channels(phase):
        for way in (RIGHT, LEFT):
            send_one(phase, way)

    def forward(phase):
        if relayed:
            @pl.when(rad == 3)
            def _():
                to_relay(phase, DOWN_HI).wait_recv()
                remote(relay.at[phase], above.at[phase, high], phase, FORWARD, DOWN_HI, target[UP]).start()

            @pl.when(rad == 0)
            def _():
                to_relay(phase, UP_HI).wait_recv()
                remote(relay.at[phase], below.at[phase, high], phase, FORWARD, UP_HI, target[DOWN]).start()

    def receive_channels(phase):
        for way in (RIGHT, LEFT):
            @pl.when(has[opposite[way]])
            def _():
                copy_of(phase, way).wait_recv()

    def receive_rows(phase):
        for way, other in ((DOWN, UP), (UP, DOWN), (DOWN_HI, UP), (UP_HI, DOWN)):
            @pl.when(has[other])
            def _():
                copy_of(phase, way).wait_recv()

    def wait_sent(phase):
        for way, needs in ((RIGHT, RIGHT), (LEFT, LEFT), (DOWN, DOWN), (UP, UP), (DOWN_HI, DOWN), (UP_HI, UP)):
            @pl.when(has[needs])
            def _():
                copy_of(phase, way).wait_send()
        if relayed:
            @pl.when(jnp.logical_or(rad == 0, rad == 3))
            def _():
                remote(relay.at[phase], above.at[phase, high], phase, FORWARD, DOWN_HI, across).wait_send()

    row = lax.broadcasted_iota(jnp.int32, (nrows, ncols), 0)
    col = lax.broadcasted_iota(jnp.int32, (nrows, ncols), 1)
    radius_one = radius_start + grid_step * (rad * nrows + row).astype(jnp.float32)
    radius_two = radius_start + grid_step * col.astype(jnp.float32)
    greater = jnp.maximum(radius_one, radius_two)
    lesser = jnp.minimum(radius_one, radius_two)
    forms[0] = radius_one
    forms[1] = radius_two
    forms[2] = 1.0 / greater
    forms[3] = lesser / (greater * greater)
    forms[4] = 0.5 / (radius_one * radius_one)
    forms[5] = 0.5 / (radius_two * radius_two)

    for edge, way in ((above, UP), (below, DOWN)):
        @pl.when(jnp.logical_not(has[way]))
        def _():
            edge[...] = jnp.zeros_like(edge)

    def turn(value, amount, axis=0):
        amount %= value.shape[axis]
        return pltpu.roll(value, amount, axis) if amount else value

    def packed(value, side, k, tile):
        value = value * kinetic_scale
        if side == 0:
            rows = jnp.where(row == nrows - 2, 16.0 * turn(value, -1) - value, -value)
            rows = turn(rows, 2 * k + 2)
        else:
            rows = jnp.where(row == 1, 16.0 * turn(value, 1) - value, -value)
            rows = turn(rows, 2 * k)
        return rows if tile is None else jnp.where(row < 2 * k, tile, rows)

    def pack_rows(phase):
        ext = exts[phase]

        def step(q, carry):
            for side in range(2):
                tile = None
                for k in range(group):
                    tile = packed(ext[reach + q * group + k], side, k, tile)
                pack[phase, side, q] = tile
            return carry

        lax.fori_loop(0, nchan // group, step, 0)

    def local_part(phase, base):
        ext = exts[phase]

        def step(c, carry):
            value = ext[reach + c]
            one = angulars[0, chan_start + c].astype(jnp.float32)
            two = angulars[1, chan_start + c].astype(jnp.float32)
            near = jnp.where(col >= 1, turn(value, 1, 1), 0.0) + jnp.where(col < ncols - 1, turn(value, -1, 1), 0.0)
            near += jnp.where(row >= 1, turn(value, 1), 0.0) + jnp.where(row < nrows - 1, turn(value, -1), 0.0)
            far = jnp.where(col >= 2, turn(value, 2, 1), 0.0) + jnp.where(col < ncols - 2, turn(value, -2, 1), 0.0)
            far += jnp.where(row >= 2, turn(value, 2), 0.0) + jnp.where(row < nrows - 2, turn(value, -2), 0.0)
            kinetic = (16.0 * near - far - 60.0 * value) * kinetic_scale
            diagonal = (one * (one + 1.0)) * forms[4] + (two * (two + 1.0)) * forms[5]
            base[c] = kinetic + diagonal * value
            return carry

        lax.fori_loop(0, nchan, step, 0, unroll=group * 2)

    def coupled_part(phase, base):
        ext = exts[phase]

        def step(c, carry):
            total = base[c]
            for s in range(nentries):
                link = links[s, chan_start + c] - chan_start + reach
                picked = ext[jnp.clip(link, 0, nchan + 2 * reach - 1)]
                weight = coefs[s, chan_start + c] * forms[kinds[s, chan_start + c]]
                total += weight * picked
            base[c] = total
            return carry

        lax.fori_loop(0, nchan, step, 0, unroll=group * 2)

    def edge_part(phase, base, emit, packs=None):
        def step(q, carry):
            upper, lower = above[phase, q], below[phase, q]
            tiles = [None, None]
            for k in range(group):
                c = q * group + k
                edge = jnp.where(row < nrows // 2, turn(upper, -2 * k), turn(lower, nrows - 2 - 2 * k))
                edge = jnp.where((row < 2) | (row >= nrows - 2), edge, 0.0)
                value = emit(c, base[c] + edge)
                if packs is not None:
                    tiles = [packed(value, side, k, tiles[side]) for side in range(2)]
            if packs is not None:
                for side in range(2):
                    pack[packs, side, q] = tiles[side]
            return carry

        lax.fori_loop(0, nchan // group, step, 0)

    fills[0].wait()
    pack_rows(0)
    neighbours = sum(has[way].astype(jnp.int32) for way in range(4)) + int(relayed)
    pl.semaphore_wait(barrier, neighbours)
    send_rows(0)
    send_channels(0)
    for copy in tables:
        copy.wait()

    def emit_f1(c, total):
        value = -time_step * total
        ext_f1[reach + c] = value
        return value

    def emit_f0(c, total):
        value = time_step * total
        ext_f0[reach + c] = value
        return value

    def emit_out0(c, total):
        out_ref[0, c] = ext_w0[reach + c] + ext_f0[reach + c] + (0.5 * time_step) * total

    def emit_out1(c, total):
        out_ref[1, c] = ext_w1[reach + c] + ext_f1[reach + c] - (0.5 * time_step) * total

    local_part(0, base_a)
    fills[1].wait()
    pack_rows(1)
    local_part(1, base_b)
    forward(0)
    send_rows(1)
    send_channels(1)
    receive_channels(0)
    coupled_part(0, base_a)
    forward(1)
    receive_rows(0)
    edge_part(0, base_a, emit_f1, 2)
    send_rows(2)
    send_channels(2)
    local_part(2, base_a)
    receive_channels(1)
    coupled_part(1, base_b)
    forward(2)
    receive_rows(1)
    edge_part(1, base_b, emit_f0, 3)
    send_rows(3)
    send_channels(3)
    local_part(3, base_b)
    receive_channels(2)
    coupled_part(2, base_a)
    forward(3)
    receive_rows(2)
    edge_part(2, base_a, emit_out0)
    receive_channels(3)
    coupled_part(3, base_b)
    receive_rows(3)
    edge_part(3, base_b, emit_out1)
    for phase in range(4):
        wait_sent(phase)


def body(wave_field, partner, coupling_kind, coupling, angular):
    parts, nchan, nrows, ncols = wave_field.shape
    tables = (partner.T, coupling_kind.T, coupling.T, angular.T)
    reach = nchan // 2
    group = nrows // 2
    tiles = nchan // group
    f32 = jnp.float32
    ext = pltpu.VMEM((nchan + 2 * reach, nrows, ncols), f32)
    base = pltpu.VMEM((nchan, nrows, ncols), f32)
    return pl.pallas_call(
        kernel,
        out_shape=pltpu.VMEM(wave_field.shape, f32),
        in_specs=[pl.BlockSpec(memory_space=pltpu.HBM)] * 5,
        out_specs=pl.BlockSpec(memory_space=pltpu.VMEM),
        scratch_shapes=[
            *(pltpu.SMEM(table.shape, table.dtype) for table in tables),
            pltpu.VMEM((KINDS + 2, nrows, ncols), f32),
            ext, ext, ext, ext, base, base,
            pltpu.VMEM((4, 2, tiles, nrows, ncols), f32),
            pltpu.VMEM((4, tiles, nrows, ncols), f32),
            pltpu.VMEM((4, tiles, nrows, ncols), f32),
            pltpu.VMEM((4, tiles // 2, nrows, ncols), f32),
            pltpu.SemaphoreType.DMA((4,)),
            pltpu.SemaphoreType.DMA((2,)),
            pltpu.SemaphoreType.DMA((4, 8)),
            pltpu.SemaphoreType.DMA((4, 8)),
        ],
        compiler_params=pltpu.CompilerParams(
            collective_id=0, has_side_effects=True, vmem_limit_bytes=67_043_328 - 4 * wave_field.size
        ),
        name="taylor_step",
    )(*tables, wave_field)


def solution(mesh):
    placed = (P(None, "chan", "rad", None), P(), P(), P(), P())
    return jax.shard_map(
        body, mesh=mesh, in_specs=placed, out_specs=P(None, "chan", "rad", None), check_vma=False
    )
```

```python
import functools

import jax
import jax.numpy as jnp
from jax import lax
from jax.experimental import pallas as pl
from jax.experimental.pallas import tpu as pltpu
from jax.sharding import PartitionSpec as P

KINDS = 4

time_step = 0.004
grid_step = 0.2
radius_start = 1.0
kinetic_scale = -1.0 / (24.0 * grid_step * grid_step)

RIGHT, LEFT, DOWN, UP, DOWN_HI, UP_HI = range(6)
FORWARD = DOWN_HI


def kernel(
    partner_ref, kind_ref, coef_ref, angular_ref, wave_ref, out_ref,
    links, kinds, coefs, angulars, forms,
    ext_w0, ext_w1, ext_f1, ext_f0, base_a, base_b, pack, above, below, relay,
    table_sem, local_sem, send_sem, recv_sem, met_sem,
):
    nchan, nrows, ncols = wave_ref.shape[1:]
    nentries = coef_ref.shape[0]
    reach = nchan // 2
    group = nrows // 2
    chan, rad = lax.axis_index("chan"), lax.axis_index("rad")
    chans, rads = lax.axis_size("chan"), lax.axis_size("rad")
    chan_start = chan * nchan
    has = {RIGHT: chan < chans - 1, LEFT: chan > 0, DOWN: rad < rads - 1, UP: rad > 0}
    target = {
        RIGHT: {"chan": chan + 1}, LEFT: {"chan": chan - 1},
        DOWN: {"rad": rad + 1}, UP: {"rad": rad - 1},
    }
    opposite = {RIGHT: LEFT, LEFT: RIGHT, DOWN: UP, UP: DOWN}
    own = pl.ds(reach, nchan)
    exts = (ext_w0, ext_w1, ext_f1, ext_f0)

    relayed = rads == 4
    ends, mids = jnp.logical_or(rad == 0, rad == 3), jnp.logical_or(rad == 1, rad == 2)
    across = {"rad": lax.rem(rad + 2, rads)}
    meets = dict(has)
    if relayed:
        meets[DOWN] = jnp.logical_or(rad == 0, rad == 2)
        meets[UP] = jnp.logical_or(rad == 1, rad == 3)

    barrier = pltpu.get_barrier_semaphore()
    for way in range(4):
        @pl.when(meets[way])
        def _():
            pl.semaphore_signal(
                barrier, inc=1, device_id=target[way], device_id_type=pl.DeviceIdType.MESH
            )
    if relayed:
        pl.semaphore_signal(barrier, inc=1, device_id=across, device_id_type=pl.DeviceIdType.MESH)

    fills = [
        pltpu.make_async_copy(wave_ref.at[p], exts[p].at[own], local_sem.at[p]) for p in range(2)
    ]
    tables = [
        pltpu.make_async_copy(src, dst, table_sem.at[i])
        for i, (src, dst) in enumerate(
            ((partner_ref, links), (kind_ref, kinds), (coef_ref, coefs), (angular_ref, angulars))
        )
    ]
    for copy in fills + tables:
        copy.start()

    def remote(source, dest, phase, sent, received, device):
        return pltpu.make_async_remote_copy(
            src_ref=source, dst_ref=dest,
            send_sem=send_sem.at[sent], recv_sem=recv_sem.at[phase, received],
            device_id=device, device_id_type=pl.DeviceIdType.MESH,
        )

    tiles = nchan // group
    half = tiles // 2
    low, high = pl.ds(0, half), pl.ds(half, half)
    halves = ((0, half), (half, tiles))
    lines = ((DOWN, UP), (DOWN_HI, UP_HI))

    def copy_of(phase, way):
        ext = exts[phase]
        if way == RIGHT:
            source = wave_ref.at[phase, pl.ds(reach, reach)] if phase < 2 else ext.at[pl.ds(nchan, reach)]
            return remote(source, ext.at[pl.ds(0, reach)], phase, way, way, target[way])
        if way == LEFT:
            source = wave_ref.at[phase, pl.ds(0, reach)] if phase < 2 else ext.at[pl.ds(reach, reach)]
            return remote(source, ext.at[pl.ds(reach + nchan, reach)], phase, way, way, target[way])
        down = way in (DOWN, DOWN_HI)
        part = low if way in (DOWN, UP) else high
        edge = above if down else below
        toward = DOWN if down else UP
        return remote(pack.at[1 - down, phase, part], edge.at[phase, part], phase, toward, way, target[toward])

    def to_relay(phase, way):
        side, received = (0, UP_HI) if way == DOWN_HI else (1, DOWN_HI)
        return remote(pack.at[side, phase, high], relay.at[phase], phase, (DOWN, UP)[side], received, across)

    def send_far(phase, part):
        if relayed:
            @pl.when(rad == 1)
            def _():
                copy_of(phase, DOWN).start() if part == 0 else to_relay(phase, DOWN_HI).start()

            @pl.when(rad == 2)
            def _():
                copy_of(phase, UP).start() if part == 0 else to_relay(phase, UP_HI).start()

    def send_near(phase, part):
        for way, toward in zip(lines[part], (DOWN, UP)):
            @pl.when(meets[toward])
            def _():
                copy_of(phase, way).start()

    def send_channel(phase, way):
        @pl.when(has[way])
        def _():
            copy_of(phase, way).start()

    def forward(phase):
        if relayed:
            @pl.when(rad == 3)
            def _():
                to_relay(phase, DOWN_HI).wait_recv()
                remote(relay.at[phase], above.at[phase, high], phase, FORWARD, DOWN_HI, target[UP]).start()

            @pl.when(rad == 0)
            def _():
                to_relay(phase, UP_HI).wait_recv()
                remote(relay.at[phase], below.at[phase, high], phase, FORWARD, UP_HI, target[DOWN]).start()

    def receive_channels(phase):
        for way in (RIGHT, LEFT):
            @pl.when(has[opposite[way]])
            def _():
                copy_of(phase, way).wait_recv()

    def receive_rows(phase, part):
        for way, other in zip(lines[part], (UP, DOWN)):
            @pl.when(has[other])
            def _():
                copy_of(phase, way).wait_recv()

    def wait_sent():
        for way, whole in (
            (RIGHT, ext_w0.at[pl.ds(0, 4 * reach)]), (LEFT, ext_w0.at[pl.ds(0, 4 * reach)]),
            (DOWN, pack.at[0]), (UP, pack.at[1]),
        ):
            @pl.when(has[way])
            def _():
                remote(whole, whole, 0, way, way, target[way]).wait_send()
        if relayed:
            @pl.when(ends)
            def _():
                remote(relay, relay, 0, FORWARD, DOWN_HI, across).wait_send()

    row = lax.broadcasted_iota(jnp.int32, (nrows, ncols), 0)
    col = lax.broadcasted_iota(jnp.int32, (nrows, ncols), 1)
    radius_one = radius_start + grid_step * (rad * nrows + row).astype(jnp.float32)
    radius_two = radius_start + grid_step * col.astype(jnp.float32)
    greater = jnp.maximum(radius_one, radius_two)
    lesser = jnp.minimum(radius_one, radius_two)
    forms[0] = radius_one
    forms[1] = radius_two
    forms[2] = 1.0 / greater
    forms[3] = lesser / (greater * greater)
    forms[4] = 0.5 / (radius_one * radius_one)
    forms[5] = 0.5 / (radius_two * radius_two)

    for edge, way in ((above, UP), (below, DOWN)):
        @pl.when(jnp.logical_not(has[way]))
        def _():
            edge[...] = jnp.zeros_like(edge)

    def turn(value, amount, axis=0):
        amount %= value.shape[axis]
        return pltpu.roll(value, amount, axis) if amount else value

    def packed(value, side, k, tile):
        value = value * kinetic_scale
        if side == 0:
            rows = jnp.where(row == nrows - 2, 16.0 * turn(value, -1) - value, -value)
            rows = turn(rows, 2 * k + 2)
        else:
            rows = jnp.where(row == 1, 16.0 * turn(value, 1) - value, -value)
            rows = turn(rows, 2 * k)
        return rows if tile is None else jnp.where(row < 2 * k, tile, rows)

    def pack_rows(phase):
        ext = exts[phase]

        def step(q, carry):
            for side in range(2):
                tile = None
                for k in range(group):
                    tile = packed(ext[reach + q * group + k], side, k, tile)
                pack[side, phase, q] = tile
            return carry

        lax.fori_loop(0, nchan // group, step, 0)

    def local_part(phase, base):
        ext = exts[phase]

        def step(c, carry):
            value = ext[reach + c]
            one = angulars[0, chan_start + c].astype(jnp.float32)
            two = angulars[1, chan_start + c].astype(jnp.float32)
            near = jnp.where(col >= 1, turn(value, 1, 1), 0.0) + jnp.where(col < ncols - 1, turn(value, -1, 1), 0.0)
            near += jnp.where(row >= 1, turn(value, 1), 0.0) + jnp.where(row < nrows - 1, turn(value, -1), 0.0)
            far = jnp.where(col >= 2, turn(value, 2, 1), 0.0) + jnp.where(col < ncols - 2, turn(value, -2, 1), 0.0)
            far += jnp.where(row >= 2, turn(value, 2), 0.0) + jnp.where(row < nrows - 2, turn(value, -2), 0.0)
            kinetic = (16.0 * near - far - 60.0 * value) * kinetic_scale
            diagonal = (one * (one + 1.0)) * forms[4] + (two * (two + 1.0)) * forms[5]
            base[c] = kinetic + diagonal * value
            return carry

        lax.fori_loop(0, nchan, step, 0, unroll=group * 2)

    def coupled_part(phase, base):
        ext = exts[phase]

        def step(c, carry):
            total = base[c]
            for s in range(nentries):
                link = links[s, chan_start + c] - chan_start + reach
                picked = ext[jnp.clip(link, 0, nchan + 2 * reach - 1)]
                weight = coefs[s, chan_start + c] * forms[kinds[s, chan_start + c]]
                total += weight * picked
            base[c] = total
            return carry

        lax.fori_loop(0, nchan, step, 0, unroll=group * 2)

    def edge_part(phase, part, base, emit, packs=None):
        def step(q, carry):
            upper, lower = above[phase, q], below[phase, q]
            tiles = [None, None]
            for k in range(group):
                c = q * group + k
                edge = jnp.where(row < nrows // 2, turn(upper, -2 * k), turn(lower, nrows - 2 - 2 * k))
                edge = jnp.where((row < 2) | (row >= nrows - 2), edge, 0.0)
                value = emit(c, base[c] + edge)
                if packs is not None:
                    tiles = [packed(value, side, k, tiles[side]) for side in range(2)]
            if packs is not None:
                for side in range(2):
                    pack[side, packs, q] = tiles[side]
            return carry

        lax.fori_loop(*halves[part], step, 0)

    fills[0].wait()
    pack_rows(0)
    partners = sum(meets[way].astype(jnp.int32) for way in range(4)) + int(relayed)
    pl.semaphore_wait(barrier, partners)
    if relayed:
        for here, there in ((0, 1), (3, 2)):
            @pl.when(rad == here)
            def _():
                pl.semaphore_signal(
                    met_sem, inc=1, device_id={"rad": there}, device_id_type=pl.DeviceIdType.MESH
                )
    send_far(0, 1)
    send_near(0, 0)
    send_near(0, 1)
    send_channel(0, RIGHT)
    send_channel(0, LEFT)
    fills[1].wait()
    pack_rows(1)
    if relayed:
        @pl.when(mids)
        def _():
            pl.semaphore_wait(met_sem, 1)
    send_far(0, 0)
    send_far(1, 0)
    send_far(1, 1)
    send_near(1, 0)
    for copy in tables:
        copy.wait()

    def emit_f1(c, total):
        value = -time_step * total
        ext_f1[reach + c] = value
        return value

    def emit_f0(c, total):
        value = time_step * total
        ext_f0[reach + c] = value
        return value

    def emit_out0(c, total):
        out_ref[0, c] = ext_w0[reach + c] + ext_f0[reach + c] + (0.5 * time_step) * total

    def emit_out1(c, total):
        out_ref[1, c] = ext_w1[reach + c] + ext_f1[reach + c] - (0.5 * time_step) * total

    def advance(phase, base, emit):
        for part in range(2):
            receive_rows(phase, part)
            edge_part(phase, part, base, emit, phase + 2)
            send_far(phase + 2, part)
            send_near(phase + 2, part)
            send_channel(phase + 2, (LEFT, RIGHT)[part])

    def finish(phase, base, emit):
        for part in range(2):
            receive_rows(phase, part)
            edge_part(phase, part, base, emit)

    local_part(0, base_a)
    forward(0)
    send_near(1, 1)
    send_channel(1, RIGHT)
    send_channel(1, LEFT)
    local_part(1, base_b)
    forward(1)
    receive_channels(0)
    coupled_part(0, base_a)
    advance(0, base_a, emit_f1)
    local_part(2, base_a)
    receive_channels(1)
    coupled_part(1, base_b)
    advance(1, base_b, emit_f0)
    forward(2)
    local_part(3, base_b)
    receive_channels(2)
    coupled_part(2, base_a)
    forward(3)
    receive_channels(3)
    coupled_part(3, base_b)
    finish(2, base_a, emit_out0)
    finish(3, base_b, emit_out1)
    wait_sent()


def body(wave_field, partner, coupling_kind, coupling, angular):
    parts, nchan, nrows, ncols = wave_field.shape
    tables = (partner.T, coupling_kind.T, coupling.T, angular.T)
    reach = nchan // 2
    group = nrows // 2
    tiles = nchan // group
    f32 = jnp.float32
    ext = pltpu.VMEM((nchan + 2 * reach, nrows, ncols), f32)
    base = pltpu.VMEM((nchan, nrows, ncols), f32)
    return pl.pallas_call(
        kernel,
        out_shape=pltpu.VMEM(wave_field.shape, f32),
        in_specs=[pl.BlockSpec(memory_space=pltpu.HBM)] * 5,
        out_specs=pl.BlockSpec(memory_space=pltpu.VMEM),
        scratch_shapes=[
            *(pltpu.SMEM(table.shape, table.dtype) for table in tables),
            pltpu.VMEM((KINDS + 2, nrows, ncols), f32),
            ext, ext, ext, ext, base, base,
            pltpu.VMEM((2, 4, tiles, nrows, ncols), f32),
            pltpu.VMEM((4, tiles, nrows, ncols), f32),
            pltpu.VMEM((4, tiles, nrows, ncols), f32),
            pltpu.VMEM((4, tiles // 2, nrows, ncols), f32),
            pltpu.SemaphoreType.DMA((4,)),
            pltpu.SemaphoreType.DMA((2,)),
            pltpu.SemaphoreType.DMA((5,)),
            pltpu.SemaphoreType.DMA((4, 6)),
            pltpu.SemaphoreType.REGULAR,
        ],
        compiler_params=pltpu.CompilerParams(
            collective_id=0, has_side_effects=True, vmem_limit_bytes=67_043_328 - 4 * wave_field.size
        ),
        name="taylor_step",
    )(*tables, wave_field)


def solution(mesh):
    placed = (P(None, "chan", "rad", None), P(), P(), P(), P())
    return jax.shard_map(
        body, mesh=mesh, in_specs=placed, out_specs=P(None, "chan", "rad", None), check_vma=False
    )
```
